32 devices in a mesh: dp: 16 (over z, y, x), seq: 2 (over core).
Axes of the slice: x: 2, y: 2, z: 4, core: 2. Of those that a mesh axis runs over, the one named last changes fastest.
Arguments:
- block_in: bfloat16 [16, 256, 768], P('dp', 'seq'), may hold values from -6 to 6
- doc_ids: int32 [16, 256], P('dp', 'seq'), may hold values from 0 to 1, as said below
- positions: int32 [16, 256], P('dp', 'seq'), may hold values from 0 to 223, as said below
- ln1_gain: bfloat16 [768], P(('dp', 'seq')), may hold values from 0.5 to 1.5
- ln1_bias: bfloat16 [768], P(('dp', 'seq')), may hold values from -3 to 3
- qkv_weight: bfloat16 [768, 2304], P(('dp', 'seq')), as said below
- qkv_bias: bfloat16 [2304], P(('dp', 'seq')), may hold values from -3 to 3
- attn_weight: bfloat16 [768, 768], P(('dp', 'seq')), may hold values from -0.875 to 0.875
- attn_bias: bfloat16 [768], P(('dp', 'seq')), may hold values from -3 to 3
- ln2_gain: bfloat16 [768], P(('dp', 'seq')), may hold values from 0.5 to 1.5
- ln2_bias: bfloat16 [768], P(('dp', 'seq')), may hold values from -3 to 3
- fc_weight: bfloat16 [768, 3072], P(('dp', 'seq')), may hold values from -0.21875 to 0.21875
- fc_bias: bfloat16 [3072], P(('dp', 'seq')), may hold values from -3 to 3
- proj_weight: bfloat16 [3072, 768], P(('dp', 'seq')), may hold values from -0.109375 to 0.109375
- proj_bias: bfloat16 [768], P(('dp', 'seq')), may hold values from -3 to 3
- grad_out: bfloat16 [16, 256, 768], P('dp', 'seq'), may hold values from -6 to 6
Outputs:
- block_out: bfloat16 [16, 256, 768], P('dp', 'seq')
- grad_in: bfloat16 [16, 256, 768], P('dp', 'seq')
- grad_ln1_gain: float32 [768], P(('dp', 'seq'))
- grad_ln1_bias: float32 [768], P(('dp', 'seq'))
- grad_qkv_weight: float32 [768, 2304], P(('dp', 'seq'))
- grad_qkv_bias: float32 [2304], P(('dp', 'seq'))
- grad_attn_weight: float32 [768, 768], P(('dp', 'seq'))
- grad_attn_bias: float32 [768], P(('dp', 'seq'))
- grad_ln2_gain: float32 [768], P(('dp', 'seq'))
- grad_ln2_bias: float32 [768], P(('dp', 'seq'))
- grad_fc_weight: float32 [768, 3072], P(('dp', 'seq'))
- grad_fc_bias: float32 [3072], P(('dp', 'seq'))
- grad_proj_weight: float32 [3072, 768], P(('dp', 'seq'))
- grad_proj_bias: float32 [768], P(('dp', 'seq'))
The draws below stay inside these ranges and needn't reach their ends.
Inputs may be any that keep to these rules, and one draw needn't show every extreme that they name: `doc_ids`: each row holds two documents: id 0 on its first tokens and id 1 on the rest; the first has 32 to 224 tokens. `positions`: each token's index within its document. `qkv_weight`: columns are the query, key and value projections in that order, each with its heads side by side.
All inputs are finite; a program needn't handle non-finite values.
Results may differ from the reference program's by a relative error of at most 0.009.
Values may be sent and summed in bfloat16 or wider, within the bound.
No kernel may reach another device: no remote copies, remote signals or barrier semaphores. Data moves between devices by JAX's collectives and lax.ppermute only.
A program may use at most 192 MiB of HBM per device.

```python
import math
import jax
import jax.numpy as jnp
from jax import lax

D = 768
HEADS = 12
HEAD = 64
ROT = 16
FF = 3072
ROW_LEN = 256
ROWS = 16


def layout(key):
    folded = jax.random.fold_in(key, 11)
    boundary = jax.random.randint(folded, (ROWS, 1), ROW_LEN // 8, 7 * ROW_LEN // 8 + 1).astype(jnp.int32)
    row_index = jnp.arange(ROWS, dtype=jnp.int32)[:, None]
    boundary = jnp.where(row_index == 0, ROW_LEN // 8, boundary).astype(jnp.int32)
    indices = jnp.arange(ROW_LEN, dtype=jnp.int32)[None, :]
    second = (indices >= boundary).astype(jnp.int32)
    within = jnp.where(second == 1, indices - boundary, indices + 0 * boundary)
    return (second, within.astype(jnp.int32))


def draw_doc_ids(key, part):
    return layout(key)[0]


def draw_positions(key, part):
    return layout(key)[1]


def draw_qkv_weight(key, part):
    drawn = jax.random.normal(key, (D, 3 * D), jnp.float32) * D ** (-0.5)
    return drawn.astype(jnp.bfloat16)


def strengthened(values, stream_key, source, target, parts, factor):
    owner, partner = [(jnp.arange(values.shape[dim]) // (values.shape[dim] // parts)).reshape([-1 if axis == dim else 1 for axis in range(values.ndim)]) for dim in (source, target)]
    chosen = jax.random.permutation(stream_key, parts)[partner]
    strong = (owner == chosen) | (owner == (partner + parts // 2) % parts)
    return jnp.where(strong, factor * values, values)


def block_levels(key, extent, pieces, smallest, largest):
    gain, own = 1.0, jax.random.fold_in(key, 6)
    for dim, parts in pieces:
        draws = jnp.exp(jax.random.uniform(jax.random.fold_in(own, dim), (parts,), jnp.float32, smallest / len(pieces), largest / len(pieces)))
        gain = gain * jnp.repeat(draws, extent[dim] // parts).reshape([-1 if axis == dim else 1 for axis in range(len(extent))])
    return gain


def scatter_about(own_key, dims, deviation, most, pieces=(), held_as=jnp.bfloat16):
    values = jax.random.normal(own_key, dims, jnp.float32) * deviation
    if len(pieces) > 0:
        values = block_levels(own_key, dims, pieces, -0.22, 0.18) * values
    return jnp.clip(values, min=-most, max=most).astype(held_as)


def gaussian_with(own_key, dims, deviation, most, pieces, heavy, kind=jnp.bfloat16):
    array = deviation * jax.random.normal(own_key, dims, jnp.float32)
    if pieces:
        array = array * block_levels(own_key, dims, pieces, -0.22, 0.18)
    return jnp.clip(strengthened(array, jax.random.fold_in(own_key, 3), *heavy), -most, most).astype(kind)


def setup_inputs(seed: int = 0) -> dict:
    key_of = jax.random.split(jax.random.key(seed), 17)
    return {
        "block_in": scatter_about(key_of[0], (ROWS, ROW_LEN, D), 1.0, 6.0, ((0, 16), (1, 2))),
        "doc_ids": draw_doc_ids(jax.random.fold_in(key_of[16], 71), 0),
        "positions": draw_positions(jax.random.fold_in(key_of[16], 71), 0),
        "ln1_gain": jnp.clip(1.0 + 0.1 * jax.random.normal(key_of[3], (D,), jnp.float32), 0.5, 1.5).astype(jnp.bfloat16),
        "ln1_bias": scatter_about(key_of[4], (D,), 0.3, 3.0, ((0, 32),)),
        "qkv_weight": draw_qkv_weight(jax.random.fold_in(key_of[16], 71), 0),
        "qkv_bias": scatter_about(key_of[6], (3 * D,), 0.3, 3.0, ((0, 32),)),
        "attn_weight": scatter_about(key_of[7], (D, D), (D // 16) ** -0.5, 0.875, ((0, 32),)),
        "attn_bias": scatter_about(key_of[8], (D,), 0.3, 3.0, ((0, 32),)),
        "ln2_gain": jnp.clip(1.0 + 0.1 * jax.random.normal(key_of[9], (D,), jnp.float32), 0.5, 1.5).astype(jnp.bfloat16),
        "ln2_bias": scatter_about(key_of[10], (D,), 0.3, 3.0, ((0, 32),)),
        "fc_weight": scatter_about(key_of[11], (D, FF), D ** -0.5, 0.21875, ((0, 32),)),
        "fc_bias": scatter_about(key_of[12], (FF,), 0.3, 3.0, ((0, 32),)),
        "proj_weight": scatter_about(key_of[13], (FF, D), FF ** -0.5, 0.109375, ((0, 32),)),
        "proj_bias": scatter_about(key_of[14], (D,), 0.3, 3.0, ((0, 32),)),
        "grad_out": gaussian_with(key_of[15], (ROWS, ROW_LEN, D), 1.0, 6.0, ((0, 16), (1, 2)), (0, 2, 16, 2.0)),
    }


EPSILON = 1e-05
ROOT_HALF = 1.0 / math.sqrt(2.0)
ROOT_TWO_PI = 1.0 / math.sqrt(2.0 * math.pi)

def layer_norm(values):
    centred = values - lax.optimization_barrier(jnp.mean(values, -1, keepdims=True))
    inverse = lax.rsqrt(lax.optimization_barrier(jnp.mean(centred * centred, -1, keepdims=True)) + EPSILON)
    return (centred * inverse, inverse)

def norm_back(upstream, normed, inverse, gain_vec):
    scaled = upstream * gain_vec.astype(jnp.float32)
    return inverse * (scaled - lax.optimization_barrier(jnp.mean(scaled, -1, keepdims=True)) - normed * lax.optimization_barrier(jnp.mean(scaled * normed, -1, keepdims=True)))

def gelu_slope(pre_act):
    return 0.5 * (1.0 + lax.erf(pre_act * ROOT_HALF)) + pre_act * jnp.exp(-0.5 * pre_act * pre_act) * ROOT_TWO_PI

def tables(token_pos):
    half_rot = ROT // 2
    frequency = 10000.0 ** (-(jnp.arange(half_rot).astype(jnp.float32) * 2.0 / ROT))
    angles = token_pos.astype(jnp.float32)[:, None] * frequency[None, :]
    return (jnp.cos(angles)[:, None, :], jnp.sin(angles)[:, None, :])

def rotate(heads, cos_table, sine_table):
    half_rot = ROT // 2
    first = heads[..., :half_rot]
    second = heads[..., half_rot:ROT]
    return jnp.concatenate([first * cos_table - second * sine_table, second * cos_table + first * sine_table, heads[..., ROT:]], -1)

def unrotate(heads, cos_table, sine_table):
    half_rot = ROT // 2
    first = heads[..., :half_rot]
    second = heads[..., half_rot:ROT]
    return jnp.concatenate([first * cos_table + second * sine_table, second * cos_table - first * sine_table, heads[..., ROT:]], -1)

def bdot(left, right):
    return jnp.dot(left, right, preferred_element_type=jnp.float32)

def reference(block_in, doc_ids, positions, ln1_gain, ln1_bias, qkv_weight, qkv_bias, attn_weight, attn_bias, ln2_gain, ln2_bias, fc_weight, fc_bias, proj_weight, proj_bias, grad_out):
    params = (ln1_gain, ln1_bias, qkv_weight, qkv_bias, attn_weight, attn_bias, ln2_gain, ln2_bias, fc_weight, fc_bias, proj_weight, proj_bias)
    score_scale = HEAD ** (-0.5)
    float_type = jnp.float32

    def one_row(totals, row_data):
        row_in, row_docs, row_pos, row_grad = row_data
        length = row_in.shape[0]
        inputs = row_in.astype(float_type)
        normed, inverse = layer_norm(inputs)
        acts1 = (normed * ln1_gain.astype(float_type) + ln1_bias.astype(float_type)).astype(jnp.bfloat16)
        acts2 = (normed * ln2_gain.astype(float_type) + ln2_bias.astype(float_type)).astype(jnp.bfloat16)
        projected = bdot(acts1, qkv_weight) + qkv_bias.astype(float_type)
        cos_table, sine_table = tables(row_pos)
        queries = rotate(projected[:, :D].reshape(length, HEADS, HEAD), cos_table, sine_table).astype(jnp.bfloat16)
        key_heads = rotate(projected[:, D:2 * D].reshape(length, HEADS, HEAD), cos_table, sine_table).astype(jnp.bfloat16)
        value_heads = projected[:, 2 * D:].reshape(length, HEADS, HEAD).astype(jnp.bfloat16)
        order = jnp.arange(length)
        allowed = (order[None, :] <= order[:, None]) & (row_docs[None, :] == row_docs[:, None])

        def scores_of():
            raw_scores = jnp.einsum('qhd,khd->hqk', queries.astype(float_type), key_heads.astype(float_type)) * score_scale
            return jnp.where(allowed[None], raw_scores, -jnp.inf)
        scores = scores_of()
        row_max = lax.optimization_barrier(jnp.max(scores, -1, keepdims=True))
        logsum = row_max + jnp.log(lax.optimization_barrier(jnp.sum(jnp.exp(scores - row_max), -1, keepdims=True)))
        probs = jnp.exp(scores - logsum).astype(jnp.bfloat16)
        context = jnp.einsum('hqk,khd->qhd', probs.astype(float_type), value_heads.astype(float_type)).astype(jnp.bfloat16).reshape(length, D)
        pre_act = bdot(acts2, fc_weight) + fc_bias.astype(float_type)
        hidden = jax.nn.gelu(pre_act, approximate=False).astype(jnp.bfloat16)
        attn_out = bdot(context, attn_weight) + attn_bias.astype(float_type)
        mlp_out = bdot(hidden, proj_weight) + proj_bias.astype(float_type)
        row_out = (inputs + attn_out + mlp_out).astype(jnp.bfloat16)
        upstream = row_grad.astype(float_type)
        grad_proj_bias = lax.optimization_barrier(jnp.sum(upstream, 0))
        grad_attn_bias = lax.optimization_barrier(jnp.sum(upstream, 0))
        grad_proj_weight = bdot(hidden.T, row_grad)
        grad_attn_weight = bdot(context.T, row_grad)
        d_pre = bdot(row_grad, proj_weight.T) * gelu_slope(pre_act)
        grad_fc_bias = lax.optimization_barrier(jnp.sum(d_pre, 0))
        d_pre_b = d_pre.astype(jnp.bfloat16)
        grad_fc_weight = bdot(acts2.T, d_pre_b)
        d_acts2 = bdot(d_pre_b, fc_weight.T)
        grad_ln2_gain = lax.optimization_barrier(jnp.sum(d_acts2 * normed, 0))
        grad_ln2_bias = lax.optimization_barrier(jnp.sum(d_acts2, 0))
        d_context = bdot(row_grad, attn_weight.T).astype(jnp.bfloat16).reshape(length, HEADS, HEAD)
        row_dot = lax.optimization_barrier(jnp.sum(d_context.astype(float_type) * context.reshape(length, HEADS, HEAD).astype(float_type), -1))
        scores = scores_of()
        weights_full = jnp.exp(scores - logsum)
        d_weights = jnp.einsum('qhd,khd->hqk', d_context.astype(float_type), value_heads.astype(float_type))
        d_scores = (weights_full * (d_weights - row_dot.T[:, :, None]) * score_scale).astype(jnp.bfloat16)
        d_query = jnp.einsum('hqk,khd->qhd', d_scores.astype(float_type), key_heads.astype(float_type))
        d_keys = jnp.einsum('hqk,qhd->khd', d_scores.astype(float_type), queries.astype(float_type))
        d_values = jnp.einsum('hqk,qhd->khd', probs.astype(float_type), d_context.astype(float_type))
        d_projected = jnp.concatenate([unrotate(d_query, cos_table, sine_table).reshape(length, D), unrotate(d_keys, cos_table, sine_table).reshape(length, D), d_values.reshape(length, D)], 1)
        grad_qkv_bias = lax.optimization_barrier(jnp.sum(d_projected, 0))
        d_proj_b = d_projected.astype(jnp.bfloat16)
        grad_qkv_weight = bdot(acts1.T, d_proj_b)
        d_acts1 = bdot(d_proj_b, qkv_weight.T)
        grad_ln1_gain = lax.optimization_barrier(jnp.sum(d_acts1 * normed, 0))
        grad_ln1_bias = lax.optimization_barrier(jnp.sum(d_acts1, 0))
        row_grad_in = (upstream + norm_back(d_acts1, normed, inverse, ln1_gain) + norm_back(d_acts2, normed, inverse, ln2_gain)).astype(jnp.bfloat16)
        local_grads = (grad_ln1_gain, grad_ln1_bias, grad_qkv_weight, grad_qkv_bias, grad_attn_weight, grad_attn_bias, grad_ln2_gain, grad_ln2_bias, grad_fc_weight, grad_fc_bias, grad_proj_weight, grad_proj_bias)
        totals = tuple((total + part_grad for total, part_grad in zip(totals, local_grads)))
        return (totals, (row_out, row_grad_in))
    zeros = tuple((jnp.zeros(param.shape, jnp.float32) for param in params))
    totals, outputs = lax.scan(one_row, zeros, (block_in, doc_ids, positions, grad_out))
    return (outputs[0], outputs[1], totals[0], totals[1], totals[2], totals[3], totals[4], totals[5], totals[6], totals[7], totals[8], totals[9], totals[10], totals[11])
```

```python
import functools
import math

import jax
import jax.numpy as jnp
from jax import lax
from jax.experimental import pallas as pl
from jax.experimental.pallas import tpu as pltpu
from jax.sharding import Mesh, PartitionSpec as P


HEADS = 12
HEAD = 64
ROT = 16

EPSILON = 1e-05
ROOT_HALF = 1.0 / math.sqrt(2.0)
ROOT_TWO_PI = 1.0 / math.sqrt(2.0 * math.pi)

F32 = jnp.float32
BF16 = jnp.bfloat16


def shifted(value, axis, by):
    count = lax.axis_size(axis)
    return lax.ppermute(value, axis, [(i, (i - by) % count) for i in range(count)])


def exchange(blocks, axis):
    return lax.all_to_all(blocks, axis, 0, 0)


def after(value, *others):
    return lax.optimization_barrier((value,) + others)[0]


def swapped(value):
    cores = lax.axis_size("c")
    return lax.ppermute(value, "c", [(i, cores - 1 - i) for i in range(cores)])


def around(value):
    ranks = lax.axis_size("r")
    mine = [value] + [shifted(value, "r", by) for by in range(1, ranks)]
    return mine, [swapped(block) for block in mine]


def in_order(mine, other):
    first = lax.axis_index("c") == 0
    mine, other = jnp.stack(mine), jnp.stack(other)
    both = jnp.stack([jnp.where(first, mine, other), jnp.where(first, other, mine)], 1)
    return jnp.roll(both, lax.axis_index("r"), 0)


def order_body(ranks, split, place_ref, *refs):
    blocks, outs = refs[: 2 * ranks], refs[2 * ranks :]
    core, rank = place_ref[0], place_ref[1]
    for by in range(ranks):
        spot = lax.rem(rank + by, ranks)
        for (start, count), out in zip(split, outs):
            mine = blocks[by][..., start : start + count, :].astype(F32)
            other = blocks[ranks + by][..., start : start + count, :].astype(F32)
            low = jnp.where(core == 0, mine, other)
            high = jnp.where(core == 0, other, mine)
            pair = jnp.concatenate([low, high], -2).astype(BF16)
            rows = pl.ds(pl.multiple_of(spot * 2 * count, 16), 2 * count)
            if pair.ndim == 2:
                out[rows, :] = pair
            else:
                for i in range(pair.shape[0]):
                    out[i, rows, :] = pair[i]


def pair_summed(blocks, axis):
    core = lax.axis_index("c")
    kept = lax.dynamic_index_in_dim(blocks, core, axis, keepdims=False)
    given = lax.dynamic_index_in_dim(blocks, 1 - core, axis, keepdims=False)
    return kept + swapped(given.astype(BF16)).astype(F32)


def summed(blocks, axis):
    count = lax.axis_size(axis)
    if count > MOST:
        return jnp.sum(exchange(blocks, axis).astype(F32), 0)
    spot = lax.axis_index(axis)
    total = lax.dynamic_index_in_dim(blocks, spot, 0, keepdims=False).astype(F32)
    for by in range(1, count):
        given = lax.dynamic_index_in_dim(blocks, (spot + by) % count, 0, keepdims=False)
        total = total + shifted(given, axis, -by).astype(F32)
    return total


def times(left, right, contract):
    return lax.dot_general(left, right, ((contract[:1], contract[1:]), ((), ())),
                           preferred_element_type=F32)


def kernel_call(body, outs, flops, scratch=(), scalars=0):
    def run(*operands):
        moved = sum(math.prod(a.shape) * a.dtype.itemsize for a in (*operands, *outs))
        return pl.pallas_call(
            body,
            out_shape=outs,
            in_specs=[pl.BlockSpec(memory_space=pltpu.SMEM)] * scalars
            + [pl.BlockSpec(memory_space=pltpu.VMEM)] * (len(operands) - scalars),
            out_specs=tuple(pl.BlockSpec(memory_space=pltpu.VMEM) for _ in outs),
            scratch_shapes=scratch,
            cost_estimate=pl.CostEstimate(flops=flops, bytes_accessed=moved, transcendentals=0),
        )(*operands)

    return run


def shape(*dims, dtype=F32):
    return jax.ShapeDtypeStruct(dims, dtype)


def pack_body(lines, part, units, count, qkv_ref, fc_ref, small_ref, out_ref):
    third = lines * part
    share = qkv_ref.shape[0]
    small = small_ref[...].astype(F32)
    lane = lax.broadcasted_iota(jnp.int32, (share, small.shape[1]), 1)
    row = lax.broadcasted_iota(jnp.int32, (share, small.shape[1]), 0)
    column = lax.broadcasted_iota(jnp.int32, (share, LANES), 1)
    table = jnp.zeros((share, LANES), F32)
    for j in range(count):
        chosen = jnp.where(lane == row + j * share, small, 0.0)
        table = jnp.where(column == j, jnp.sum(chosen, 1, keepdims=True), table)
    for i in range(lines):
        for kind in range(3):
            start = kind * third + i * part
            out_ref[i, :, kind * part : (kind + 1) * part] = qkv_ref[:, start : start + part]
        out_ref[i, :, 3 * part : 3 * part + units] = fc_ref[:, i * units : (i + 1) * units]
        out_ref[i, :, 3 * part + units :] = table.astype(BF16)


def picked(table, at, row, first):
    depth, width = table.shape[1], at.shape[1]
    chosen = lax.broadcasted_iota(jnp.int32, (depth, width), 0) == at
    values = times(table.astype(BF16), chosen.astype(F32).astype(BF16), (1, 0))
    here = lax.broadcasted_iota(jnp.int32, values.shape, 0) == row + first
    return jnp.sum(jnp.where(here, values, 0.0), 0, keepdims=True)


def turned(chunk, cos_table, sine_table):
    lane = lax.broadcasted_iota(jnp.int32, chunk.shape, 1) % HEAD
    width = chunk.shape[1]
    other = jnp.where(
        lane < ROT // 2, pltpu.roll(chunk, width - ROT // 2, 1), pltpu.roll(chunk, ROT // 2, 1)
    )
    return chunk * cos_table + other * sine_table


LANES = 128
MOST = 4


def project_body(own, part, pieces, x_refs, rest):
    (weights_ref, at_q_ref, row_q_ref, at_f_ref, row_f_ref, frequency_ref,
     qkv_ref, acts1_ref, acts2_ref, normed_ref, cos_ref, sine_ref, place_ref, vectors_ref) = rest
    columns = weights_ref.shape[1]
    table = weights_ref[:, columns - LANES :].astype(F32).T
    qkv_vec = picked(table[:16], at_q_ref[...], row_q_ref[...], 6)
    fc_vec = picked(table[:16], at_f_ref[...], row_f_ref[...], 9)
    vectors_ref[0:6] = table[0:6]
    vectors_ref[6:7] = fc_vec
    for i in range(pieces):
        rows = slice(i * own, (i + 1) * own)
        x = x_refs[i][0:own].astype(F32)
        centred = x - jnp.mean(x, -1, keepdims=True)
        normed = centred * lax.rsqrt(jnp.mean(centred * centred, -1, keepdims=True) + EPSILON)
        normed_ref[rows] = normed
        acts1_ref[rows] = (normed * table[0:1] + table[1:2]).astype(BF16)
        acts2_ref[rows] = (normed * table[2:3] + table[3:4]).astype(BF16)
        place = x_refs[i][own : own + 8, 0:own].astype(F32)[0:1]
        angle = frequency_ref[...] * place
        cosine, sine = jnp.cos(angle), jnp.sin(angle)
        ones = jnp.ones((HEAD - ROT, own), F32)
        cos_head = [cosine, cosine, ones]
        sine_head = [-sine, sine, ones * 0.0]
        cos_ref[rows] = jnp.concatenate(cos_head * (LANES // HEAD), 0).T
        sine_ref[rows] = jnp.concatenate(sine_head * (LANES // HEAD), 0).T
        place_ref[rows] = jnp.broadcast_to(place, (LANES, own)).T
    projected = times(acts1_ref[...], weights_ref[:, : 3 * part], (1, 0)) + qkv_vec
    for start in range(0, 2 * part, LANES):
        lanes = slice(start, start + LANES)
        qkv_ref[:, lanes] = turned(projected[:, lanes], cos_ref[...], sine_ref[...]).astype(BF16)
    qkv_ref[:, 2 * part :] = projected[:, 2 * part :].astype(BF16)


def hidden_body(part, acts2_ref, weights_ref, proj_ref, vectors_ref, hidden_ref, slope_ref, out_ref):
    units = proj_ref.shape[0]
    pre_act = times(acts2_ref[...], weights_ref[:, 3 * part : 3 * part + units], (1, 0))
    pre_act = pre_act + vectors_ref[6:7]
    below = 0.5 * (1.0 + lax.erf(pre_act * ROOT_HALF))
    hidden_ref[...] = (pre_act * below).astype(BF16)
    slope_ref[...] = below + pre_act * jnp.exp(-0.5 * pre_act * pre_act) * ROOT_TWO_PI
    out_ref[...] = times(hidden_ref[...], proj_ref[...], (1, 0))


def both_halves(prev_ref, own_ref, i, start):
    lanes = slice(start, start + HEAD)
    return jnp.concatenate([prev_ref[i, :, lanes], own_ref[i, :, lanes]], 0)


def attend_body(own, heads, qkv_ref, prev_ref, place_ref, mat_ref, mlp_ref,
                probs_ref, context_ref, first_ref, *rest):
    part = heads * HEAD
    pieces, out_ref = rest[:-1], rest[-1]
    key = lax.broadcasted_iota(jnp.int32, (own, 2 * own), 1) - own
    query = lax.broadcasted_iota(jnp.int32, (own, 2 * own), 0)

    @pl.loop(0, qkv_ref.shape[0])
    def _(i):
        place = jnp.broadcast_to(place_ref[i][:, 0:1], (own, 2 * own)).astype(jnp.int32)
        allowed = (key <= query) & (key >= query - place)
        for head in range(heads):
            start = head * HEAD
            keys = both_halves(prev_ref, qkv_ref, i, part + start)
            values = both_halves(prev_ref, qkv_ref, i, 2 * part + start)
            scores = times(qkv_ref[i, :, start : start + HEAD], keys, (1, 1)) * HEAD ** (-0.5)
            scores = jnp.where(allowed, scores, -jnp.inf)
            top = jnp.max(scores, -1, keepdims=True)
            logsum = top + jnp.log(jnp.sum(jnp.exp(scores - top), -1, keepdims=True))
            weights = jnp.exp(scores - logsum)
            probs_ref[i, head] = weights
            context_ref[i, :, start : start + HEAD] = times(
                weights.astype(BF16), values, (1, 0)
            ).astype(BF16)
        total = times(context_ref[i], mat_ref[...], (1, 0)) + mlp_ref[i]
        out_ref[i] = total.astype(BF16)

        @pl.when(i == 0)
        def _():
            first_ref[...] = total

    for i, piece in enumerate(pieces):
        piece[...] = out_ref[i + 1]


def dealt(core, values, kept_ref, given_ref, i, row, start, count):
    low = values[start : start + count]
    high = values[start + count : start + 2 * count]
    rows = slice(row, row + count)
    kept_ref[i, rows] = jnp.where(core == 0, low, high)
    given_ref[i, rows] = jnp.where(core == 0, high, low).astype(BF16)


def halves(values):
    high = values.astype(BF16).astype(F32)
    return high, values - high


def hidden_back_body(part, lines, own, dims, *refs):
    place_ref, refs = refs[0], refs[1:]
    (hidden_ref, slope_ref, acts2_ref, weights_ref, proj_ref, vectors_ref, normed_ref, context_ref,
     sums_ref, e_ref, grad_ref, *rest) = refs[lines:]
    if dims:
        kept_ref, given_ref, grad_proj_ref, grad_fc_ref, grad_mat_ref, unit_ref = rest
    else:
        grad_proj_ref, grad_fc_ref, grad_mat_ref, unit_ref = rest
    units = proj_ref.shape[0]
    for i in range(lines):
        grad_ref[i * own : (i + 1) * own] = refs[i][...]
    grad = grad_ref[...]
    grad_mat_ref[...] = times(context_ref[...], grad, (0, 0))
    d_pre = times(grad, proj_ref[...], (1, 1)) * slope_ref[...]
    unit_ref[0:1] = jnp.sum(d_pre, 0, keepdims=True)
    d_pre = d_pre.astype(BF16)
    grad_proj_ref[...] = times(hidden_ref[...], grad, (0, 0))
    grad_fc_ref[...] = times(acts2_ref[...], d_pre, (0, 0))
    d_acts2 = times(d_pre, weights_ref[:, 3 * part : 3 * part + units], (1, 1))
    sums_ref[0:1] = jnp.sum(d_acts2 * normed_ref[...], 0, keepdims=True)
    sums_ref[1:2] = jnp.sum(d_acts2, 0, keepdims=True)
    sums_ref[2:3] = jnp.sum(refs[0][...].astype(F32), 0, keepdims=True)
    e_ref[...] = d_acts2 * vectors_ref[2:3]
    if dims:
        ranks, share, hidden_share = dims
        core = place_ref[0]
        row = lax.broadcasted_iota(jnp.int32, (8, units), 0)
        unit = jnp.broadcast_to(unit_ref[0:1], (8, units))
        high, low = halves(unit)
        base = hidden_share + share
        for i in range(ranks):
            dealt(core, grad_proj_ref, kept_ref, given_ref, i, 0, 2 * i * hidden_share,
                  hidden_share)
            dealt(core, grad_mat_ref, kept_ref, given_ref, i, hidden_share, 2 * i * share, share)
            kept_ref[i, base : base + 8] = jnp.where(row == 0, unit, 0.0)
            given_ref[i, base : base + 8] = jnp.where(
                row == 0, high, jnp.where(row == 1, low, 0.0)
            ).astype(BF16)
            for j in range(lines):
                dealt(core, grad_fc_ref, kept_ref, given_ref, i, base + 8 + j * share,
                      (j * ranks + i) * 2 * share, share)


def fold_body(ranks, start, step, place_ref, kept_ref, got_ref, own_ref, *sent):
    rank = place_ref[1]
    for by in range(ranks):
        spot = lax.rem(rank + by, ranks)
        total = kept_ref[spot] + got_ref[spot].astype(F32)
        if by == 0:
            own_ref[...] = total
        else:
            sent[by - 1][...] = total.astype(BF16)
            if step == 1:
                value = total[start : start + 8]
                value = value[0:1] + value[1:2]
                row = lax.broadcasted_iota(jnp.int32, (8, value.shape[1]), 0)
                high, low = halves(jnp.broadcast_to(value, row.shape))
                value = jnp.where(row == 0, high, jnp.where(row == 1, low, 0.0))
                sent[by - 1][start : start + 8] = value.astype(BF16)
            else:
                value = total[start : start + step] + total[start + step : start + 2 * step]
                high, low = halves(value)
                sent[by - 1][start : start + step] = high.astype(BF16)
                sent[by - 1][start + step : start + 2 * step] = low.astype(BF16)


def lower_body(lines, share, hidden_share, own_ref, *refs):
    *got, proj_ref, mat_ref, unit_ref, swap_ref = refs
    total = own_ref[...]
    for ref in got:
        total = total + ref[...].astype(F32)
    base = hidden_share + share
    proj_ref[...] = total[:hidden_share]
    mat_ref[...] = total[hidden_share:base]
    unit_ref[...] = total[base : base + 1] + total[base + 1 : base + 2]
    for j in range(lines):
        start = base + 8 + j * share
        swap_ref[j] = total[start : start + share].astype(BF16)


def upper_body(lines, share, part, own_ref, *refs):
    *got, swap_ref, high_ref, low_ref = refs
    total = own_ref[...]
    for ref in got:
        total = total + ref[...].astype(F32)
    base = lines * share
    value = total[base : base + 16] + total[base + 16 : base + 32]
    high, low = halves(value)
    high_ref[...] = jnp.zeros_like(high_ref)
    low_ref[...] = jnp.zeros_like(low_ref)
    for j in range(lines):
        for source, target in ((high, high_ref), (low, low_ref)):
            for v in range(5):
                at, lane = 2 * v + j * part // (2 * part), (j % 2) * part
                target[v : v + 1, :part] = source[at : at + 1, lane : lane + part]
            target[5:6] = source[10:11]
        swap_ref[j, 0:8] = high_ref[...].astype(BF16)
        swap_ref[j, 8:16] = low_ref[...].astype(BF16)
        swap_ref[j, 16:] = total[j * share : (j + 1) * share].astype(BF16)


def land_body(part, got_ref, out_ref, sums_ref, row_ref):
    lines = got_ref.shape[0]
    third = lines * part
    sums = jnp.zeros((8, part), F32)
    for j in range(lines):
        value = got_ref[j, 0:8].astype(F32) + got_ref[j, 8:16].astype(F32)
        sums = sums + value[:, :part]
        for kind in range(3):
            source = slice(kind * part, (kind + 1) * part)
            target = slice(kind * third + j * part, kind * third + (j + 1) * part)
            out_ref[:, target] = got_ref[j, 16:, source].astype(F32)
            row_ref[:, target] = value[5:6, source]
    sums_ref[...] = sums


def attend_back_body(own, heads, grad_ref, qkv_ref, prev_ref, probs_ref, context_ref, mat_ref,
                     d_own_ref, d_prev_ref, d_context_ref):
    part = heads * HEAD
    scale = HEAD ** (-0.5)

    @pl.loop(0, qkv_ref.shape[0])
    def _(i):
        d_context_ref[...] = times(grad_ref[i], mat_ref[...], (1, 1)).astype(BF16)
        for head in range(heads):
            start = head * HEAD
            lanes = slice(start, start + HEAD)
            keys = both_halves(prev_ref, qkv_ref, i, part + start)
            values = both_halves(prev_ref, qkv_ref, i, 2 * part + start)
            d_context = d_context_ref[:, lanes]
            row_dot = jnp.sum(
                d_context.astype(F32) * context_ref[i, :, lanes].astype(F32), -1, keepdims=True
            )
            weights = probs_ref[i, head]
            d_scores = weights * (times(d_context, values, (1, 1)) - row_dot) * scale
            d_scores = d_scores.astype(BF16)
            d_keys = times(d_scores, qkv_ref[i, :, lanes], (0, 0))
            d_values = times(weights.astype(BF16), d_context, (0, 0))
            d_own_ref[i, :, lanes] = times(d_scores, keys, (1, 0))
            d_own_ref[i, :, part + start : part + start + HEAD] = d_keys[own:]
            d_own_ref[i, :, 2 * part + start : 2 * part + start + HEAD] = d_values[own:]
            d_prev_ref[i, :, lanes] = d_keys[:own].astype(BF16)
            d_prev_ref[i, :, part + start : part + start + HEAD] = d_values[:own].astype(BF16)


def project_back_body(own, part, lines, dims, place_ref, sums2_ref, d_own_ref, back_ref, cos_ref, sine_ref, acts1_ref, weights_ref,
                      vectors_ref, normed_ref, e_ref, first_ref, *rest):
    pieces, rest = rest[: lines - 1], rest[lines - 1 :]
    if dims:
        kept_ref, given_ref, grad_ref, sums_ref, column_ref, whole_ref, d_ref, extra_ref = rest
    else:
        grad_ref, sums_ref, column_ref, whole_ref, d_ref = rest
    whole_ref[...] = d_own_ref[...]
    whole_ref[:, part:] += back_ref[...].astype(F32)
    for start in range(0, 2 * part, LANES):
        lanes = slice(start, start + LANES)
        whole_ref[:, lanes] = turned(whole_ref[:, lanes], cos_ref[...], -sine_ref[...])
    column_ref[0:1] = jnp.sum(whole_ref[...], 0, keepdims=True)
    d_ref[...] = whole_ref[...].astype(BF16)
    d_acts1 = times(d_ref[...], weights_ref[:, : 3 * part], (1, 1))
    sums_ref[0:1] = jnp.sum(d_acts1 * normed_ref[...], 0, keepdims=True)
    sums_ref[1:2] = jnp.sum(d_acts1, 0, keepdims=True)
    total = d_acts1 * vectors_ref[0:1] + e_ref[...]
    first_ref[...] = total[:own]
    for i, piece in enumerate(pieces):
        piece[...] = total[(i + 1) * own : (i + 2) * own].astype(BF16)
    grad_ref[...] = times(acts1_ref[...], d_ref[...], (0, 0))
    if dims:
        ranks, share = dims
        core = place_ref[0]
        extra_ref[...] = jnp.zeros_like(extra_ref)
        wide = 2 * part
        vectors = (sums_ref[0:1], sums_ref[1:2], sums2_ref[0:1], sums2_ref[1:2], sums2_ref[2:3])
        for v, vector in enumerate(vectors):
            extra_ref[2 * v : 2 * v + 1, :wide] = vector[:, :wide]
            extra_ref[2 * v + 1 : 2 * v + 2, :wide] = vector[:, wide:]
        extra_ref[10:11] = column_ref[0:1]
        high, low = halves(extra_ref[...])
        base = lines * share
        for i in range(ranks):
            for j in range(lines):
                dealt(core, grad_ref, kept_ref, given_ref, i, j * share,
                      (j * ranks + i) * 2 * share, share)
            kept_ref[i, base : base + 16] = extra_ref[...]
            kept_ref[i, base + 16 : base + 32] = jnp.zeros_like(high)
            given_ref[i, base : base + 16] = high.astype(BF16)
            given_ref[i, base + 16 : base + 32] = low.astype(BF16)


def finish_body(count, x_ref, grad_ref, first_ref, *rest):
    total = first_ref[...]
    for i in range(count):
        total = total + rest[i][...].astype(F32)
    x = x_ref[...].astype(F32)
    centred = x - jnp.mean(x, -1, keepdims=True)
    inverse = lax.rsqrt(jnp.mean(centred * centred, -1, keepdims=True) + EPSILON)
    normed = centred * inverse
    rest[count][...] = (
        grad_ref[...].astype(F32)
        + inverse
        * (
            total
            - jnp.mean(total, -1, keepdims=True)
            - normed * jnp.mean(total * normed, -1, keepdims=True)
        )
    ).astype(BF16)


def two_parts(values):
    high = lax.reduce_precision(values, 8, 7)
    return jnp.concatenate([high, lax.reduce_precision(values - high, 8, 7)], -1)


def joined(row, size):
    return row[..., :size] + row[..., size : 2 * size]


def padded(values, width):
    return jnp.pad(values, [(0, 0)] * (values.ndim - 1) + [(0, width - values.shape[-1])])


def local(
    block_in,
    doc_ids,
    positions,
    ln1_gain,
    ln1_bias,
    qkv_weight,
    qkv_bias,
    attn_weight,
    attn_bias,
    ln2_gain,
    ln2_bias,
    fc_weight,
    fc_bias,
    proj_weight,
    proj_bias,
    grad_out,
):
    lines, ranks, cores = (lax.axis_size(axis) for axis in ("m", "r", "c"))
    row_count, local_len, width = block_in.shape
    own = row_count * local_len
    tokens = lines * own
    heads = HEADS // lines
    part = heads * HEAD
    share = qkv_weight.shape[0]
    hidden_share = proj_weight.shape[0]
    units = fc_weight.shape[1] // lines
    third = qkv_weight.shape[1] // 3
    columns = 3 * part + units

    vectors = [ln1_gain, ln1_bias, ln2_gain, ln2_bias, attn_bias, proj_bias, qkv_bias, fc_bias]
    length = sum(v.shape[0] for v in vectors)
    count = length // share
    length = -(-length // LANES) * LANES
    small, start = jnp.zeros((1, length), BF16), 0
    for v in vectors:
        end = start + v.shape[0]
        small = small + jnp.pad(v[None], ((0, 0), (start, length - end)))
        start = end
    packed = kernel_call(
        functools.partial(pack_body, lines, part, units, count),
        (shape(lines, share, columns + LANES, dtype=BF16),),
        0,
    )(qkv_weight, fc_weight, small)[0]
    packed = exchange(packed, "m")
    lower = jnp.concatenate([proj_weight, attn_weight], 0)
    split = ((0, hidden_share), (hidden_share, share))
    where = jnp.stack([lax.axis_index("c"), lax.axis_index("r")]).astype(jnp.int32)
    fast = ranks <= MOST and share % 8 == 0 and lines == 4
    if not fast:
        lower = in_order(*around(lower))
        proj_mat = lower[:, :, :hidden_share].reshape(units, width)
        out_mat = lower[:, :, hidden_share:].reshape(part, width)
        weights = in_order(*around(packed)).transpose(2, 0, 1, 3, 4)
    else:

        def ordered(split, outs, mine, other):
            return kernel_call(
                functools.partial(order_body, ranks, split), outs, 0, scalars=1
            )(where, *mine, *other)

        proj_mat, out_mat = ordered(
            split, (shape(units, width, dtype=BF16), shape(part, width, dtype=BF16)), *around(lower)
        )
        weights = ordered(
            ((0, share),),
            (shape(lines, width // lines, columns + LANES, dtype=BF16),),
            *around(packed),
        )[0]
    weights = weights.reshape(width, columns + LANES)
    line = lax.axis_index("m")
    spot = jnp.arange(3 * part)
    spot = (spot // part) * third + line * part + spot % part
    per = qkv_bias.shape[0]
    at_q = ((spot // per) * share + spot % share)[None]
    row_q = ((spot % per) // share)[None]
    spot = line * units + jnp.arange(units)
    per = fc_bias.shape[0]
    at_f = ((spot // per) * share + spot % share)[None]
    row_f = ((spot % per) // share)[None]
    frequency = 10000.0 ** (-(jnp.arange(ROT // 2).astype(F32) * 2.0 / ROT))
    frequency = jnp.broadcast_to(frequency[:, None], (ROT // 2, own))

    own_in = block_in.reshape(own, width)
    own_grad = grad_out.reshape(own, width)
    place = padded(positions.reshape(1, own).astype(BF16), width)
    sent = jnp.concatenate([own_in, jnp.broadcast_to(place, (8, width))], 0)
    arrived = [sent] + [shifted(sent, "m", by) for by in range(1, lines)]
    late_grad = after(own_grad, weights)
    grads = [own_grad] + [shifted(late_grad, "m", by) for by in range(1, lines)]

    def project(*refs):
        project_body(own, part, lines, refs[:lines], refs[lines:])

    qkv, acts1, acts2, normed, cosine, sine, place, vectors = kernel_call(
        project,
        (
            shape(tokens, 3 * part, dtype=BF16),
            shape(tokens, width, dtype=BF16),
            shape(tokens, width, dtype=BF16),
            shape(tokens, width),
            shape(tokens, LANES),
            shape(tokens, LANES),
            shape(tokens, LANES),
            shape(8, width),
        ),
        2 * tokens * width * 3 * part,
    )(*arrived, weights, at_q, row_q, at_f, row_f, frequency)
    qkv = qkv.reshape(lines, own, 3 * part)
    prev = lax.ppermute(qkv, "c", [(i, i + 1) for i in range(cores - 1)])
    hidden, slope, mlp_out = kernel_call(
        functools.partial(hidden_body, part),
        (shape(tokens, units, dtype=BF16), shape(tokens, units), shape(tokens, width)),
        4 * tokens * width * units,
    )(acts2, weights, proj_mat, vectors)
    probs, context, first, *outward = kernel_call(
        functools.partial(attend_body, own, heads),
        (
            shape(lines, heads, own, 2 * own),
            shape(lines, own, part, dtype=BF16),
            shape(own, width),
            *[shape(own, width, dtype=BF16)] * (lines - 1),
        ),
        8 * tokens * own * part,
        [pltpu.VMEM((lines, own, width), BF16)],
    )(qkv, prev, place.reshape(lines, own, LANES), out_mat, mlp_out.reshape(lines, own, width))
    block_sum = first
    for by in range(1, lines):
        block_sum = block_sum + shifted(outward[by - 1], "m", -by).astype(F32)
    block_out = (own_in.astype(F32) + block_sum + (vectors[4] + vectors[5])).astype(BF16)

    grads = after(tuple(grads), first)
    base = hidden_share + share + 8
    plain = (
        shape(units, width),
        shape(width, units),
        shape(part, width),
        shape(8, units),
    )
    dealt_rows = base + lines * share
    sums2, e_hidden, grads, *given1 = kernel_call(
        functools.partial(
            hidden_back_body, part, lines, own, (ranks, share, hidden_share) if fast else None
        ),
        (
            shape(8, width),
            shape(tokens, width),
            shape(tokens, width, dtype=BF16),
            *(
                (
                    shape(ranks, dealt_rows, width),
                    shape(ranks, dealt_rows, width, dtype=BF16),
                )
                if fast
                else plain
            ),
        ),
        8 * tokens * width * units,
        [pltpu.VMEM(a.shape, a.dtype) for a in plain] if fast else [],
        scalars=1,
    )(where, *grads, hidden, slope, acts2, weights, proj_mat, vectors, normed,
      context.reshape(tokens, part))
    if fast:
        got1 = swapped(given1[1])
    d_own, d_prev = kernel_call(
        functools.partial(attend_back_body, own, heads),
        (
            shape(lines, own, 3 * part),
            shape(lines, own, 2 * part, dtype=BF16),
        ),
        16 * tokens * own * part,
        [pltpu.VMEM((own, part), BF16)],
    )(grads.reshape(lines, own, width), qkv, prev, probs, context, out_mat)
    back = lax.ppermute(d_prev, "c", [(i + 1, i) for i in range(cores - 1)])
    if fast:
        own1, *sent1 = kernel_call(
            functools.partial(fold_body, ranks, hidden_share + share, 1),
            (
                shape(dealt_rows, width),
                *[shape(dealt_rows, width, dtype=BF16)] * (ranks - 1),
            ),
            0,
            scalars=1,
        )(where, given1[0], after(got1, back))
        got1 = [shifted(sent1[by - 1], "r", -by) for by in range(1, ranks)]
    plain = (shape(width, 3 * part), shape(8, width), shape(8, 3 * part))
    dealt_rows = lines * share + 32
    first, *rest = kernel_call(
        functools.partial(
            project_back_body, own, part, lines, (ranks, share) if fast else None
        ),
        (
            shape(own, width),
            *[shape(own, width, dtype=BF16)] * (lines - 1),
            *(
                (
                    shape(ranks, dealt_rows, 3 * part),
                    shape(ranks, dealt_rows, 3 * part, dtype=BF16),
                )
                if fast
                else plain
            ),
        ),
        4 * tokens * width * 3 * part,
        ([pltpu.VMEM(a.shape, a.dtype) for a in plain] if fast else [])
        + [pltpu.VMEM((tokens, 3 * part), F32), pltpu.VMEM((tokens, 3 * part), BF16)]
        + ([pltpu.VMEM((16, 3 * part), F32)] if fast else []),
        scalars=1,
    )(
        where, sums2, d_own.reshape(tokens, 3 * part), back.reshape(tokens, 2 * part), cosine, sine, acts1,
        weights, vectors, normed, e_hidden,
    )
    outward, given2 = rest[: lines - 1], rest[lines - 1 :]
    grad_in = kernel_call(
        functools.partial(finish_body, lines - 1), (shape(own, width, dtype=BF16),), 0
    )(own_in, own_grad, first, *[shifted(outward[by - 1], "m", -by) for by in range(1, lines)])[0]
    block_out = block_out.reshape(row_count, local_len, width)
    grad_in = grad_in.reshape(row_count, local_len, width)
    if fast:
        out_proj, out_attn, unit, swap = kernel_call(
            functools.partial(lower_body, lines, share, hidden_share),
            (
                shape(hidden_share, width),
                shape(share, width),
                shape(1, units),
                shape(lines, share, units, dtype=BF16),
            ),
            0,
        )(own1, *got1)
        rank, core = lax.axis_index("r"), lax.axis_index("c")
        spot = rank * cores + core
        out_fc_vec = lax.dynamic_slice_in_dim(unit[0], spot * hidden_share, hidden_share, 0)
        swap = exchange(swap, "m")
        out_fc = swap.transpose(1, 0, 2).reshape(share, lines * units).astype(F32)
        got2 = swapped(given2[1])
        own2, *sent2 = kernel_call(
            functools.partial(fold_body, ranks, lines * share, 16),
            (
                shape(dealt_rows, 3 * part),
                *[shape(dealt_rows, 3 * part, dtype=BF16)] * (ranks - 1),
            ),
            0,
            scalars=1,
        )(where, given2[0], got2)
        got2 = [shifted(sent2[by - 1], "r", -by) for by in range(1, ranks)]
        swap = kernel_call(
            functools.partial(upper_body, lines, share, part),
            (shape(lines, 16 + share, 3 * part, dtype=BF16),),
            0,
            [pltpu.VMEM((8, 3 * part), F32), pltpu.VMEM((8, 3 * part), F32)],
        )(own2, *got2)[0]
        out_qkv, sums, row = kernel_call(
            functools.partial(land_body, part),
            (shape(share, 3 * third), shape(8, part), shape(1, 3 * third)),
            0,
        )(exchange(swap, "m"))
        sums = lax.dynamic_slice_in_dim(sums, spot * share, share, 1)
        per = qkv_bias.shape[0]
        spot = (line * ranks + rank) * cores + core
        out_qkv_vec = lax.dynamic_slice_in_dim(row[0], spot * per, per, 0)
        return (
            block_out, grad_in, sums[0], sums[1], out_qkv, out_qkv_vec, out_attn, sums[4],
            sums[2], sums[3], out_fc, out_fc_vec, out_proj, sums[4],
        )

    grad_proj, grad_fc, grad_attn, unit_sums = given1
    grad_qkv, sums1, columns_sum = given2
    grad_fc_vec, grad_qkv_vec = unit_sums[0], columns_sum[0]
    grad_gain1, grad_bias1, grad_gain2, grad_bias2 = sums1[0], sums1[1], sums2[0], sums2[1]
    grad_sum = sums2[2]

    lower = pair_summed(
        jnp.concatenate(
            [
                grad_attn.reshape(ranks, cores, share, width),
                grad_proj.reshape(ranks, cores, hidden_share, width),
                padded(two_parts(grad_fc_vec.reshape(ranks, cores, 1, hidden_share)), width),
            ],
            2,
        ),
        1,
    )
    lower = jnp.concatenate(
        [lower[:, :-1], padded(two_parts(joined(lower[:, -1:], hidden_share)), width)], 1
    )
    lower = summed(lower.astype(BF16), "r")
    out_attn = lower[:share]
    out_proj = lower[share:-1]
    out_fc_vec = joined(lower[-1], hidden_share)

    upper = pair_summed(grad_fc.reshape(lines, ranks, cores, share, units), 2)
    upper = summed(upper.astype(BF16).transpose(1, 0, 2, 3), "r")
    upper = exchange(upper.astype(BF16), "m")
    out_fc = upper.transpose(1, 0, 2).reshape(share, lines * units).astype(F32)

    spots = jnp.zeros((3, third), F32)
    spots = lax.dynamic_update_slice(spots, grad_qkv_vec.reshape(3, part), (0, line * part))
    extras = jnp.concatenate(
        [
            vector.reshape(lines, ranks, cores, -1)
            for vector in (grad_gain1, grad_bias1, grad_gain2, grad_bias2, grad_sum, spots)
        ],
        -1,
    )[:, :, :, None]
    size = extras.shape[-1]
    upper = jnp.concatenate(
        [
            grad_qkv.reshape(lines, ranks, cores, share, 3 * part),
            padded(two_parts(extras), 3 * part),
        ],
        3,
    )

    def repacked(sums):
        return jnp.concatenate(
            [sums[..., :share, :], padded(two_parts(joined(sums[..., share:, :], size)), 3 * part)],
            -2,
        ).astype(BF16)

    upper = repacked(pair_summed(upper, 2)).transpose(1, 0, 2, 3)
    upper = exchange(repacked(summed(upper, "r")), "m").astype(F32)
    out_qkv = upper[:, :share].reshape(lines, share, 3, part).transpose(1, 2, 0, 3)
    out_qkv = out_qkv.reshape(share, 3 * third)
    extras = jnp.sum(joined(upper[:, share], size), 0)
    out_gain1, out_bias1, out_gain2, out_bias2, out_sum = (
        extras[i * share : (i + 1) * share] for i in range(5)
    )
    out_qkv_vec = extras[5 * share :]
    return (
        block_out,
        grad_in,
        out_gain1,
        out_bias1,
        out_qkv,
        out_qkv_vec,
        out_attn,
        out_sum,
        out_gain2,
        out_bias2,
        out_fc,
        out_fc_vec,
        out_proj,
        out_sum,
    )


def solution(mesh):
    lines = math.gcd(HEADS, mesh.shape["dp"])
    grid = Mesh(
        mesh.devices.reshape(lines, mesh.shape["dp"] // lines, mesh.shape["seq"]), ("m", "r", "c")
    )
    rows = P(("m", "r"), "c", None)
    marks = P(("m", "r"), "c")
    vector = P(("m", "r", "c"))
    matrix = P(("m", "r", "c"), None)

    return jax.shard_map(
        local,
        mesh=grid,
        in_specs=(
            rows, marks, marks, vector, vector, matrix, vector, matrix, vector,
            vector, vector, matrix, vector, matrix, vector, rows,
        ),
        out_specs=(
            rows, rows, vector, vector, matrix, vector, matrix, vector,
            vector, vector, matrix, vector, matrix, vector,
        ),
        check_vma=False,
    )
```
